32 devices in a mesh: eig: 2 (over x), tok: 16 (over z, y, core).
Axes of the slice: x: 2, y: 2, z: 4, core: 2. Of those that a mesh axis runs over, the one named last changes fastest.
Arguments:
- activations: bfloat16 [384, 28672], P('tok', 'eig'), may hold values from -6 to 6
- out_grads: bfloat16 [384, 8192], P('tok'), may hold values from -6 to 6
- act_basis: bfloat16 [28672, 28672], P('eig', 'tok'), may hold values from -0.03125 to 0.03125
- grad_basis: bfloat16 [8192, 8192], P('tok', 'eig'), may hold values from -0.0625 to 0.0625
- query: bfloat16 [8192, 28672], P('eig', 'tok'), may hold values from -0.00036621094 to 0.00036621094
Outputs:
- scores: float32 [384], P('tok')
The draws below stay inside these ranges and needn't reach their ends.
All inputs are finite; a program needn't handle non-finite values.
Results may differ from the reference program's by a relative error of at most 0.0031.
Values may be sent and summed in bfloat16 or wider, within the bound.
No kernel may reach another device: no remote copies, remote signals or barrier semaphores. Data moves between devices by JAX's collectives and lax.ppermute only.
A program may use at most 192 MiB of HBM per device.

```python
import jax
import jax.numpy as jnp
from jax import lax

DIN = 28672
DOUT = 8192
TOKENS = 384


def block_scale(key, extent, pieces, low, high):
    loudness = 1.0
    for dim, blocks in pieces:
        steps = jax.random.uniform(jax.random.fold_in(jax.random.fold_in(key, 6), dim), (blocks,), jnp.float32, low / len(pieces), high / len(pieces))
        loudness = loudness * jnp.repeat(jnp.exp(steps), extent[dim] // blocks).reshape((-1,) + (1,) * (len(extent) - 1 - dim))
    return loudness


def centred(stream_key, shape, scale, reach, cuts=(), kind=jnp.bfloat16):
    loudness = block_scale(stream_key, shape, cuts, -0.22, 0.18) if cuts else 1.0
    values = jax.random.normal(stream_key, shape, jnp.float32) * scale * loudness
    return jnp.minimum(jnp.maximum(values, -reach), reach).astype(kind)


def setup_inputs(seed: int = 0) -> dict:
    arg_keys = jax.random.split(jax.random.key(seed), 6)
    activations = centred(arg_keys[0], (TOKENS, DIN), 1.0, 6.0, ((0, 16), (1, 2)))
    out_grads = centred(arg_keys[1], (TOKENS, DOUT), 1.0, 6.0, ((0, 16),))
    act_basis = centred(arg_keys[2], (DIN, DIN), DIN ** -0.5, 0.03125, ((0, 2), (1, 16)))
    grad_basis = centred(arg_keys[3], (DOUT, DOUT), DOUT ** -0.5, 0.0625, ((0, 16), (1, 2)))
    query = centred(arg_keys[4], (DOUT, DIN), (DOUT * DIN) ** -0.5, 0.00036621094, ((0, 2), (1, 16)))
    return {"activations": activations, "out_grads": out_grads, "act_basis": act_basis, "grad_basis": grad_basis, "query": query}


def reference(activations, out_grads, act_basis, grad_basis, query):
    acts_wide = activations.astype(jnp.float32)
    rotated_grads = jnp.dot(out_grads.astype(jnp.float32), grad_basis.astype(jnp.float32))
    width = DIN // 8

    def step(carry, index):
        start = index * width
        basis_block = lax.dynamic_slice_in_dim(act_basis, start, width, 1).astype(jnp.float32)
        rotated = jnp.dot(acts_wide, basis_block).astype(jnp.bfloat16)
        query_block = lax.dynamic_slice_in_dim(query, start, width, 1).astype(jnp.float32)
        carry = carry + jnp.dot(rotated.astype(jnp.float32), query_block.T)
        return carry, None

    initial = jnp.zeros((TOKENS, DOUT), jnp.float32)
    projected, _ = lax.scan(step, initial, jnp.arange(8, dtype=jnp.int32))
    return jnp.sum(rotated_grads * projected, axis=1)
```

```python
import functools

import jax
import jax.numpy as jnp
from jax import lax
from jax.experimental import pallas as pl
from jax.experimental.pallas import tpu as pltpu
from jax.sharding import PartitionSpec as P

INTERPRET = False
FIRST = 5
WAIT = 0
F32 = jnp.float32
BF16 = jnp.bfloat16


def tile_of(extent):
    return next((t for t in (3584, 2048, 1024, 512, 256, 128) if extent % t == 0), extent)


def rotate_kernel(count, half_ref, *refs):
    del half_ref
    acts, basis, out = refs[:count], refs[count], refs[count + 1]
    held = jnp.concatenate([a[...] for a in acts], axis=0)
    term = jnp.dot(held, basis[...], preferred_element_type=F32)

    @pl.when(pl.program_id(0) == 0)
    def _():
        out[...] = term

    @pl.when(pl.program_id(0) > 0)
    def _():
        out[...] += term


def rotate(acts, basis, half):
    depth, width = basis.shape
    width //= 2
    rows = sum(a.shape[0] for a in acts)
    deep = tile_of(depth)
    return pl.pallas_call(
        functools.partial(rotate_kernel, len(acts)),
        out_shape=jax.ShapeDtypeStruct((rows, width), F32),
        grid_spec=pltpu.PrefetchScalarGridSpec(
            num_scalar_prefetch=1,
            grid=(depth // deep,),
            in_specs=[
                pl.BlockSpec((a.shape[0], deep), lambda k, half: (0, k)) for a in acts
            ]
            + [pl.BlockSpec((deep, width), lambda k, half: (k, half[0]))],
            out_specs=pl.BlockSpec((rows, width), lambda k, half: (0, 0)),
        ),
        compiler_params=pltpu.CompilerParams(dimension_semantics=("arbitrary",)),
        cost_estimate=pl.CostEstimate(
            flops=2 * rows * depth * width,
            bytes_accessed=2 * depth * width + 2 * rows * depth + 4 * rows * width,
            transcendentals=0,
        ),
        interpret=INTERPRET,
    )(half.reshape(1).astype(jnp.int32), *acts, basis)


def on_device(n_eig, n_tok, activations, out_grads, act_basis, grad_basis, query):
    cores = 2
    chips = n_tok // cores
    ring = list(range(0, chips, 2)) + list(range(chips - 1, 0, -2))
    onward, back = [], []
    for chip in range(chips):
        place = ring.index(chip)
        after, before = ring[(place + 1) % chips], ring[place - 1]
        onward += [(2 * chip, 2 * after), (2 * chip + 1, 2 * before + 1)]
        back += [(2 * chip, 2 * before), (2 * chip + 1, 2 * after + 1)]
    swap = [(i, i ^ 1) for i in range(n_tok)]
    flip = [(0, 1), (1, 0)]

    def forward(x):
        return lax.ppermute(x, "tok", onward)

    def backward(x):
        return lax.ppermute(x, "tok", back)

    def partner(x):
        return lax.ppermute(x, "tok", swap)

    def place_of(chip):
        return jnp.where(chip % 2 == 0, chip // 2, chips - 1 - chip // 2)

    def chip_at(place):
        return jnp.where(2 * place < chips, 2 * place, 2 * (chips - place) - 1)

    rows = activations.shape[0]
    me = lax.axis_index("tok")
    eig = lax.axis_index("eig")
    core = me % cores
    way = 1 - 2 * core
    pos = place_of(me // cores)
    n_fore = chips // 2
    n_aft = chips - 1 - n_fore
    first = chips * FIRST // 8
    s = {("a", 0): activations}
    again = []

    def ring_acts():
        for step in range(1, chips):
            s["a", step] = forward(s["a", step - 1])
            s["b", step - 1] = partner(s["a", step - 1])
            yield
        s["b", chips - 1] = partner(s["a", chips - 1])
        yield

    def ring_grads():
        cols = lax.all_to_all(out_grads, "tok", split_axis=1, concat_axis=0, tiled=True)
        yield
        s["cols"] = cols
        yield
        width = cols.shape[1]
        cols = s["cols"].reshape(chips, cores, rows, width)
        other = lax.dynamic_index_in_dim(cols, 1 - core, 1, keepdims=False)
        own = lax.dynamic_index_in_dim(cols, core, 1, keepdims=False)
        other = jnp.dot(
            other.reshape(chips * rows, width), grad_basis, preferred_element_type=F32
        )
        own = jnp.dot(
            own.reshape(chips * rows, width), grad_basis, preferred_element_type=F32
        )
        s["part"] = own + partner(other)
        yield
        for _ in range(WAIT):
            yield

        def part_at(step):
            who = chip_at((pos + way * step) % chips)
            return lax.dynamic_slice_in_dim(s["part"], who * rows, rows, 0)

        for step in range(1, n_fore + 1):
            kind = BF16 if step <= n_fore // 2 else F32
            fore = part_at(n_fore + 1 - step)
            if step > 1:
                fore = fore + s["fore"].astype(F32)
            s["fore"] = forward(fore.astype(kind))
            if step <= n_aft:
                aft = part_at(step - 1 - n_aft)
                if step > 1:
                    aft = aft + s["aft"].astype(F32)
                s["aft"] = backward(aft.astype(kind))
            yield
        total = part_at(0) + s["fore"].astype(F32) + s["aft"].astype(F32)
        s["g", 0] = total.astype(BF16)
        sent = []
        for step in range(1, n_fore + 1):
            s["g", step] = forward(s["g", step - 1])
            if step <= n_aft:
                s["g", chips - step] = backward(s["g", (chips - step + 1) % chips])
            if step == n_fore:
                swap_grads(sent)
            yield
        swap_grads(sent)
        yield

    def swap_grads(sent):
        new = [i for i in range(chips) if i not in sent and ("g", i) in ready]
        sent += new
        came = partner(jnp.concatenate([s["g", i] for i in new], axis=0))
        for at, i in enumerate(new):
            s["h", i] = came[at * rows : (at + 1) * rows]

    def rotate_chunk(chunk, steps):
        for _ in range(steps[-1] + 1):
            yield
        keys = [("a", i) for i in steps] + [("b", i) for i in steps]
        again.extend(keys)
        if n_eig == 2:
            s["yours", chunk] = rotate([s[k] for k in keys], act_basis, 1 - eig)
            yield
            came = lax.ppermute(s["yours", chunk], "eig", flip)
            s["mine", chunk] = rotate([s[k] for k in keys], act_basis, eig)
            s["came", chunk] = came
            for k in keys:
                again.remove(k)
            yield
            mine = (s["mine", chunk] + s["came", chunk]).astype(BF16)
            s["mine", chunk], s["came", chunk] = mine, lax.ppermute(mine, "eig", flip)
            yield
            mine, came = s["mine", chunk], s["came", chunk]
            left, right = jnp.where(eig == 0, mine, came), jnp.where(eig == 0, came, mine)
            s["r", chunk] = jnp.concatenate([left, right], axis=1)
        else:
            acts = jnp.concatenate([s[k] for k in keys], axis=0)
            part = jnp.dot(acts, act_basis, preferred_element_type=F32)
            s["r", chunk] = lax.psum(part, "eig").astype(BF16)
            yield

    groups = [range(first), range(first, chips)]
    tasks = [ring_acts(), ring_grads()] + [rotate_chunk(i, g) for i, g in enumerate(groups)]
    ready = dict(s)
    while tasks:
        alive = []
        for task in tasks:
            try:
                next(task)
                alive.append(task)
            except StopIteration:
                pass
        tasks = alive
        new = [k for k in s if k not in ready or s[k] is not ready[k] or k in again]
        if new and tasks:
            for k, v in zip(new, lax.optimization_barrier([s[k] for k in new])):
                s[k] = v
        ready = dict(s)

    rotated = jnp.concatenate([s["r", 0], s["r", 1]], axis=0)
    grads = jnp.concatenate([s[k, i] for g in groups for k in "gh" for i in g], axis=0)
    projected = lax.dot_general(
        rotated, query, (((1,), (1,)), ((), ())), preferred_element_type=F32
    )
    partial = jnp.sum(projected * grads.astype(F32), axis=1).reshape(n_tok, rows)
    ids = jnp.arange(n_tok, dtype=jnp.int32)
    their = place_of(ids // cores)
    mine = (ids % cores) == core
    step_of = jnp.where(mine, (pos - their) * way, (their - pos) * way) % chips
    late = step_of >= first
    source = jnp.where(mine == late, first, jnp.where(late, chips, 0)) + step_of
    pick = source[:, None] == jnp.arange(n_tok, dtype=jnp.int32)[None, :]
    ordered = jnp.sum(jnp.where(pick[:, :, None], partial[None], 0.0), axis=1)
    arrived = lax.all_to_all(ordered, "tok", split_axis=0, concat_axis=0, tiled=True)
    return lax.psum(jnp.sum(arrived, axis=0), "eig")


def solution(mesh):
    sizes = dict(mesh.shape)

    def body(*args):
        return on_device(sizes["eig"], sizes["tok"], *args)

    return jax.shard_map(
        body,
        mesh=mesh,
        in_specs=(
            P("tok", "eig"),
            P("tok", None),
            P("eig", "tok"),
            P("tok", "eig"),
            P("eig", "tok"),
        ),
        out_specs=P("tok"),
        check_vma=False,
    )
```
